768 devices in a mesh: grp: 16 (over y_hi, x, core), sub: 48 (over z, y_lo).
Axes of the slice: x: 4, y: 8 (y_hi: 2, y_lo: 4; y = y_hi * 4 + y_lo), z: 12, core: 2. Of those that a mesh axis runs over, the one named last changes fastest.
Arguments:
- loads: float32 [768, 8, 1024], P(('grp', 'sub')), may hold values from -6 to 6
- schur: bfloat16 [768, 1024, 1024], P(('grp', 'sub')), may hold values from -0.1875 to 0.1875
- neumann: bfloat16 [768, 1024, 1024], P(('grp', 'sub')), may hold values from -0.1875 to 0.1875
- basis: float32 [768, 24, 1024], P(('grp', 'sub')), may hold values from -0.375 to 0.375
- coarse_index: int32 [768, 24], P(('grp', 'sub')), may hold values from 0 to 3071
- coarse_inverse: float32 [3072, 3072], P(('grp', 'sub')), may hold values from -1 to 3
Outputs:
- solution: float32 [768, 8, 1024], P(('grp', 'sub'))
- residual: float32 [768, 8, 1024], P(('grp', 'sub'))
The draws below stay inside these ranges and needn't reach their ends.
All inputs are finite; a program needn't handle non-finite values.
Results may differ from the reference program's by a relative error of at most 0.00063.
Values sent between devices are 32-bit elements; how exact they have to be, the bound alone decides.
No kernel may reach another device: no remote copies, remote signals or barrier semaphores. Data moves between devices by JAX's collectives and lax.ppermute only.
A program may use at most 64 MiB of HBM per device.

```python
import jax
import jax.numpy as jnp
from jax import lax

IFACE = 1024
RIM = 256
NCRN = 24
LOADS = 8
ITERS = 1
SUBS = 768
COARSE = 3072
N_GRP = 16
N_SUB = 48


def draw_coarse_inverse(key, part):
    first_key, second_key = jax.random.split(jax.random.fold_in(key, 17))
    diagonal = jax.random.uniform(first_key, (COARSE,), jnp.float32, 0.5, 2.0)
    mixing = jax.random.normal(second_key, (COARSE, COARSE), jnp.float32) * (0.6 / COARSE ** 0.5)
    return jnp.diag(diagonal) + mixing


def with_ends(drawn, rng, low, top_value):
    place = [jax.random.randint(jax.random.fold_in(rng, axis), (), 0, length) for axis, length in enumerate(drawn.shape)]
    widest = drawn.shape.index(max(drawn.shape))
    beside = place[:widest] + [(place[widest] + 1) % drawn.shape[widest]] + place[widest + 1:]
    return drawn.at[tuple(place)].set(low).at[tuple(beside)].set(top_value)


def block_scale(key, extent, pieces, low, top_value):
    factor_of = 1.0
    for axis_at, parts in pieces:
        steps = jax.random.uniform(jax.random.fold_in(jax.random.fold_in(key, 6), axis_at), (parts,), jnp.float32, low / len(pieces), top_value / len(pieces))
        factor_of = factor_of * jnp.repeat(jnp.exp(steps), extent[axis_at] // parts).reshape((-1,) + (1,) * (len(extent) - 1 - axis_at))
    return factor_of


def bell_draw(key, shape, scale, bound, cuts=(), kind=jnp.bfloat16):
    loudness = block_scale(key, shape, cuts, -0.22, 0.18) if cuts else 1.0
    entries = jax.random.normal(key, shape, jnp.float32) * scale * loudness
    return jnp.minimum(jnp.maximum(entries, -bound), bound).astype(kind)


def setup_inputs(seed: int = 0) -> dict:
    arg_keys = jax.random.split(jax.random.key(seed), 7)
    loads = bell_draw(arg_keys[0], (SUBS, LOADS, IFACE), 1.0, 6.0, ((0, 768),), jnp.float32)
    schur = bell_draw(arg_keys[1], (SUBS, IFACE, IFACE), IFACE ** -0.5, 0.1875, ((0, 768),))
    neumann = bell_draw(arg_keys[2], (SUBS, IFACE, IFACE), IFACE ** -0.5, 0.1875, ((0, 768),))
    basis = bell_draw(arg_keys[3], (SUBS, NCRN, IFACE), (IFACE // 4) ** -0.5, 0.375, ((0, 768),), jnp.float32)
    coarse_index = with_ends(jax.random.randint(arg_keys[4], (SUBS, NCRN), 0, COARSE), jax.random.fold_in(arg_keys[4], 1), 0, COARSE - 1).astype(jnp.int32)
    coarse_inverse = draw_coarse_inverse(jax.random.fold_in(arg_keys[6], 71), 0)
    return dict(loads=loads, schur=schur, neumann=neumann, basis=basis, coarse_index=coarse_index, coarse_inverse=coarse_inverse)


def assemble(field):
    chains = field.reshape(N_GRP, N_SUB, LOADS, IFACE)
    zeros = jnp.zeros((N_GRP, 1, LOADS, RIM), field.dtype)
    from_left = jnp.concatenate([zeros, chains[:, :-1, :, IFACE - RIM:]], axis=1)
    from_right = jnp.concatenate([chains[:, 1:, :, :RIM], zeros], axis=1)
    middle = chains[:, :, :, RIM:IFACE - RIM]
    joined = jnp.concatenate([chains[:, :, :, :RIM] + from_left, middle, chains[:, :, :, IFACE - RIM:] + from_right], axis=3)
    return joined.reshape(field.shape)


def rim_weights(dtype):
    position = jnp.arange(N_GRP * N_SUB, dtype=jnp.int32) % N_SUB
    columns = jnp.arange(IFACE, dtype=jnp.int32)
    lower_rim = (columns[None, :] < RIM) & (position[:, None] > 0)
    upper_rim = (columns[None, :] >= IFACE - RIM) & (position[:, None] < N_SUB - 1)
    weights = jnp.where(lower_rim | upper_rim, 0.5, 1.0).astype(dtype)
    return weights[:, None, :]


def local_products(field, matrices, diagonal_scale, factor):
    def single(operands):
        vector, matrix = operands
        product = jnp.dot(vector.astype(jnp.bfloat16), matrix, preferred_element_type=jnp.float32)
        return diagonal_scale * vector + factor * product.astype(vector.dtype)
    return lax.map(single, (field, matrices))


def reference(loads, schur, neumann, basis, coarse_index, coarse_inverse):
    weights = rim_weights(loads.dtype)
    force = assemble(loads)
    high = lax.Precision.HIGHEST

    def precondition(resid):
        weighted = weights * resid
        neumann_part = local_products(weighted, neumann, 0.25, 0.0625)
        coarse_terms = jnp.einsum('sli,ski->skl', weighted, basis, precision=high)
        flat_terms = coarse_terms.reshape(SUBS * NCRN, LOADS)
        coarse_residual = jax.ops.segment_sum(flat_terms, coarse_index.reshape(-1).astype(jnp.int32), num_segments=COARSE)
        coarse_value = jnp.dot(coarse_residual.T, coarse_inverse, precision=high)
        picked = coarse_value.T[coarse_index.astype(jnp.int32)]
        coarse_part = jnp.einsum('skl,ski->sli', picked, basis, precision=high)
        return assemble(weights * (neumann_part + coarse_part))

    solution = jnp.zeros_like(loads)
    residual = force
    for sweep in range(ITERS):
        solution = solution + precondition(residual)
        residual = force - assemble(local_products(solution, schur, 4.0, 1.0))
    return solution, residual
```

```python
import jax
import jax.numpy as jnp
from jax import lax
from jax.sharding import Mesh, PartitionSpec as P

RIM = 256
ALL = ("yh", "x", "c", "z", "yl")
SIZES = (2, 4, 2, 12, 4)
CHAIN = ("z", "yl")
ROWS = ("yh", "x", "yl")
COLS = ("z", "c")
N_ROWS = 32
N_COLS = 24
LANES = 128


def exchange(x, axes):
    return lax.all_to_all(x, axes, split_axis=0, concat_axis=0, tiled=True)


def position_of(index):
    owner = index // 4
    group, member = owner // 48, owner % 48
    row_part = (group // 2) * 4 + member % 4
    col_part = (member // 4) * 2 + group % 2
    return row_part * LANES + col_part * 4 + index % 4


def local(loads, schur, neumann, basis, coarse_index, coarse_inverse):
    width = loads.shape[2]
    high = lax.Precision.HIGHEST
    peers = 48
    position = lax.axis_index(CHAIN)
    columns = lax.broadcasted_iota(jnp.int32, (1, width), 1)
    lower_rim = (columns < RIM) & (position > 0)
    upper_rim = (columns >= width - RIM) & (position < peers - 1)
    weights = jnp.where(lower_rim | upper_rim, 0.5, 1.0).astype(jnp.float32)
    up = [(i, i + 1) for i in range(peers - 1)]
    down = [(j, i) for i, j in up]

    def assemble(field):
        before = lax.ppermute(field[:, width - RIM :], CHAIN, up)
        after = lax.ppermute(field[:, :RIM], CHAIN, down)
        middle = field[:, RIM : width - RIM]
        return jnp.concatenate([field[:, :RIM] + before, middle, field[:, width - RIM :] + after], axis=1)

    index = coarse_index[0]
    owner_hot = (position_of(index)[:, None] == lax.broadcasted_iota(jnp.int32, (1, N_ROWS * LANES), 1)).astype(jnp.float32)
    value_hot = (index[:, None] == lax.broadcasted_iota(jnp.int32, (1, N_COLS * LANES), 1)).astype(jnp.float32)

    force = assemble(loads[0])
    weighted = weights * force
    product = jnp.dot(weighted.astype(jnp.bfloat16), neumann[0], preferred_element_type=jnp.float32)
    neumann_part = 0.25 * weighted + 0.0625 * product
    coarse_terms = jnp.dot(weighted, basis[0].T, precision=high)

    partial = jnp.dot(coarse_terms, owner_hot, precision=high)
    partial = partial.reshape(8, N_ROWS, LANES).transpose(1, 0, 2)
    part = exchange(partial, ROWS).sum(0)
    inverse = coarse_inverse.reshape(4, N_COLS, LANES).transpose(1, 0, 2)
    sent = jnp.concatenate(
        [jnp.broadcast_to(part, (N_COLS, 8, LANES)), inverse, jnp.zeros((N_COLS, 4, LANES), jnp.float32)], axis=1
    )
    arrived = exchange(sent, COLS)
    residual_rows = arrived[:, :8].sum(0)[:, : 4 * N_COLS]
    block = arrived[:, 8:12].reshape(4 * N_COLS, LANES)
    value_part = jnp.dot(residual_rows, block, precision=high)
    value_cols = exchange(jnp.broadcast_to(value_part, (N_ROWS, 8, LANES)), ROWS).sum(0)
    value = exchange(jnp.broadcast_to(value_cols, (N_COLS, 8, LANES)), COLS)
    value = value.transpose(1, 0, 2).reshape(8, N_COLS * LANES)
    picked = jnp.dot(value, value_hot.T, precision=high)

    combined = neumann_part + jnp.dot(picked, basis[0], precision=high)
    solution = assemble(weights * combined)
    product = jnp.dot(solution.astype(jnp.bfloat16), schur[0], preferred_element_type=jnp.float32)
    residual = force - assemble(4.0 * solution + product)
    return (solution[None], residual[None])


def solution(mesh):
    whole = Mesh(mesh.devices.reshape(SIZES), ALL)
    specs = tuple(P(ALL, *([None] * n)) for n in (2, 2, 2, 2, 1, 1))
    outs = (P(ALL, None, None), P(ALL, None, None))
    return jax.shard_map(local, mesh=whole, in_specs=specs, out_specs=outs, check_vma=False)
```

```python
import jax
import jax.numpy as jnp
from jax import lax
from jax.experimental import pallas as pl
from jax.experimental.pallas import tpu as pltpu
from jax.sharding import Mesh, PartitionSpec as P


RIM = 256
ALL = ("yh", "x", "c", "z", "yl")
SIZES = (2, 4, 2, 12, 4)
CHAIN = ("z", "yl")
ROWS = ("yh", "x", "yl")
COLS = ("z", "c")
CHAIN_LENGTH = 48
N_ROWS = 32
N_COLS = 24
SLOT_BEFORE = 32
SLOT_AFTER = 64
LANES = 128
HIGH = lax.Precision.HIGHEST
F32 = jnp.float32
BF16 = jnp.bfloat16


def exchange(x, axes):
    return lax.all_to_all(x, axes, split_axis=0, concat_axis=0, tiled=True)


def position_of(index):
    owner = index // 4
    group, member = owner // 48, owner % 48
    row_part = (group // 2) * 4 + member % 4
    col_part = (member // 4) * 2 + group % 2
    return row_part * LANES + col_part * 4 + index % 4


def three_parts(x):
    first = x.astype(BF16)
    rest = x - first.astype(F32)
    second = rest.astype(BF16)
    third = (rest - second.astype(F32)).astype(BF16)
    return jnp.concatenate([first.astype(F32), second.astype(F32), third.astype(F32)], axis=0).astype(BF16)


def added(x):
    return x[0:8] + x[8:16] + x[16:24]


def scatter_kernel(lower, middle, upper, before, after, scaled_basis, place, force, out):
    whole = jnp.concatenate([lower[...] + before[...], middle[...], upper[...] + after[...]], axis=1)
    force[...] = whole
    terms = lax.dot_general(whole, scaled_basis[...], (((1,), (1,)), ((), ())), precision=HIGH, preferred_element_type=F32)
    columns = lax.broadcasted_iota(jnp.int32, (place.shape[0], N_ROWS * LANES), 1)
    hot = (columns == place[...]).astype(F32).astype(BF16)
    dense = added(jnp.dot(three_parts(terms), hot, preferred_element_type=F32))
    for p in range(N_ROWS):
        out[p] = dense[:, p * LANES : (p + 1) * LANES]


def spread_kernel(arrived, out):
    total = jnp.sum(arrived[...], axis=0)
    out[...] = jnp.broadcast_to(total[None], out.shape)


def block_kernel(arrived, block, out):
    total = jnp.sum(arrived[...], axis=0)[:, : block.shape[0]]
    value = jnp.dot(total, block[...], precision=HIGH, preferred_element_type=F32)
    out[...] = jnp.broadcast_to(value[None], out.shape)


def finish_kernel(value, names, scaled_basis, neumann_part, before, after, schur, solution, applied, held, sems):
    width = neumann_part.shape[1]
    cases, corners = neumann_part.shape[0], scaled_basis.shape[0]
    copies = [
        pltpu.make_async_copy(schur.at[pl.ds(k * RIM, RIM)], held.at[pl.ds(k * RIM, RIM)], sems.at[k])
        for k in range(width // RIM)
    ]
    for copy in copies:
        copy.start()
    last = cases + corners
    wanted = names[...] + before[last : last + 1, :LANES] + after[last : last + 1, :LANES]
    found = jnp.zeros((3 * cases, LANES), F32)
    for q in range(N_COLS):
        rows = lax.broadcasted_iota(jnp.int32, (LANES, LANES), 0) + (q * LANES + 1)
        hot = (rows.astype(F32) == wanted).astype(F32).astype(BF16)
        found += jnp.dot(three_parts(value[q]), hot, preferred_element_type=F32)
    picked = added(found)

    def coarse(slot, basis):
        return jnp.dot(picked[:, slot : slot + corners], basis, precision=HIGH, preferred_element_type=F32)

    u = neumann_part[...] + coarse(0, scaled_basis[...])
    lower = u[:, :RIM] + before[:cases] + coarse(SLOT_BEFORE, before[cases:last])
    upper = u[:, width - RIM :] + after[:cases] + coarse(SLOT_AFTER, after[cases:last])
    u = jnp.concatenate([lower, u[:, RIM : width - RIM], upper], axis=1)
    solution[...] = u
    total = 4.0 * u
    rounded = u.astype(BF16)
    for k, copy in enumerate(copies):
        copy.wait()
        part = rounded[:, k * RIM : (k + 1) * RIM]
        total += jnp.dot(part, held[k * RIM : (k + 1) * RIM], preferred_element_type=F32)
    applied[...] = total


def call(kernel, shapes, *args, in_hbm=(), scratch=(), limit=24 << 20):
    shapes = [jax.ShapeDtypeStruct(s, F32) for s in shapes]
    return pl.pallas_call(
        kernel,
        out_shape=shapes,
        in_specs=[pl.BlockSpec(memory_space=pltpu.HBM if i in in_hbm else pltpu.VMEM) for i in range(len(args))],
        out_specs=[pl.BlockSpec(memory_space=pltpu.VMEM)] * len(shapes),
        scratch_shapes=list(scratch),
        compiler_params=pltpu.CompilerParams(vmem_limit_bytes=limit),
    )(*args)


def local(loads, schur, neumann, basis, coarse_index, coarse_inverse):
    loads, schur, neumann, basis, index = loads[0], schur[0], neumann[0], basis[0], coarse_index[0]
    cases, width = loads.shape
    corners = basis.shape[0]
    position = lax.axis_index(CHAIN)
    columns = lax.broadcasted_iota(jnp.int32, (1, width), 1)
    lower_rim = (columns < RIM) & (position > 0)
    upper_rim = (columns >= width - RIM) & (position < CHAIN_LENGTH - 1)
    weights = jnp.where(lower_rim | upper_rim, 0.5, 1.0).astype(F32)
    up = [(i, i + 1) for i in range(CHAIN_LENGTH - 1)]
    down = [(j, i) for i, j in up]

    def rims(field):
        before = lax.ppermute(field[:, width - RIM :], CHAIN, up)
        after = lax.ppermute(field[:, :RIM], CHAIN, down)
        return before, after

    def assemble(field):
        before, after = rims(field)
        middle = field[:, RIM : width - RIM]
        return jnp.concatenate([field[:, :RIM] + before, middle, field[:, width - RIM :] + after], axis=1)

    lower, middle, upper = loads[:, :RIM], loads[:, RIM : width - RIM], loads[:, width - RIM :]
    before = lax.ppermute(upper, CHAIN, up)
    after = lax.ppermute(lower, CHAIN, down)
    block = exchange(coarse_inverse.reshape(4, N_COLS, LANES).transpose(1, 0, 2), COLS).reshape(4 * N_COLS, LANES)
    place = position_of(index)[:, None]
    scaled_basis = weights * basis
    force, partial = call(
        scatter_kernel, [(cases, width), (N_ROWS, cases, LANES)], lower, middle, upper, before, after, scaled_basis, place
    )
    partial, block = lax.optimization_barrier((partial, block))
    arrived = exchange(partial, ROWS)

    weighted = weights * force
    product = jnp.dot(weighted.astype(BF16), neumann, preferred_element_type=F32)
    neumann_part = weights * (0.25 * weighted + 0.0625 * product)
    named = index.astype(F32)[None] + 1.0

    def names(slot, rows, size):
        return jnp.pad(named, ((0, rows - 1), (slot, size - slot - corners)))

    to_next = jnp.concatenate(
        [neumann_part[:, width - RIM :], scaled_basis[:, width - RIM :], names(SLOT_BEFORE, 8, RIM)], axis=0
    )
    to_last = jnp.concatenate([neumann_part[:, :RIM], scaled_basis[:, :RIM], names(SLOT_AFTER, 8, RIM)], axis=0)
    own_names = names(0, 1, LANES)
    told_before = lax.ppermute(to_next, CHAIN, up)
    told_after = lax.ppermute(to_last, CHAIN, down)

    (sent,) = call(spread_kernel, [(N_COLS, cases, LANES)], arrived)
    arrived = exchange(sent, COLS)
    arrived, own_names = lax.optimization_barrier((arrived, own_names))
    (sent,) = call(block_kernel, [(N_ROWS, cases, LANES)], arrived, block)
    arrived = exchange(sent, ROWS)
    (sent,) = call(spread_kernel, [(N_COLS, cases, LANES)], arrived)
    value = exchange(sent, COLS)
    u, applied = call(
        finish_kernel, [(cases, width), (cases, width)],
        value, own_names, scaled_basis, neumann_part, told_before, told_after, schur,
        in_hbm=(6,), limit=60 * 1024 * 1024, scratch=(pltpu.VMEM(schur.shape, BF16), pltpu.SemaphoreType.DMA((width // RIM,))),
    )
    residual = force - assemble(applied)
    return (u[None], residual[None])


def solution(mesh):
    whole = Mesh(mesh.devices.reshape(SIZES), ALL)
    specs = tuple(P(ALL, *([None] * n)) for n in (2, 2, 2, 2, 1, 1))
    outs = (P(ALL, None, None), P(ALL, None, None))
    return jax.shard_map(local, mesh=whole, in_specs=specs, out_specs=outs, check_vma=False)
```

```python
import jax
import jax.numpy as jnp
from jax import lax
from jax.experimental import pallas as pl
from jax.experimental.pallas import tpu as pltpu
from jax.sharding import Mesh, PartitionSpec as P


RIM = 256
ALL = ("yh", "x", "c", "z", "yl")
SIZES = (2, 4, 2, 12, 4)
CHAIN = ("z", "yl")
ROWS = ("yh", "x", "yl")
COLS = ("z", "c")
CHAIN_LENGTH = 48
N_ROWS = 32
N_COLS = 24
SLOT_BEFORE = 32
SLOT_AFTER = 64
LIMIT = 53 << 20
LANES = 128
HIGH = lax.Precision.HIGHEST
F32 = jnp.float32
BF16 = jnp.bfloat16


def exchange(x, axes):
    return lax.all_to_all(x, axes, split_axis=0, concat_axis=0, tiled=True)


def position_of(index):
    owner = index // 4
    group, member = owner // 48, owner % 48
    row_part = (group // 2) * 4 + member % 4
    col_part = (member // 4) * 2 + group % 2
    return row_part * LANES + col_part * 4 + index % 4


def three_parts(x):
    first = x.astype(BF16)
    rest = x - first.astype(F32)
    second = rest.astype(BF16)
    third = (rest - second.astype(F32)).astype(BF16)
    return jnp.concatenate([first.astype(F32), second.astype(F32), third.astype(F32)], axis=0).astype(BF16)


def added(x):
    return x[0:8] + x[8:16] + x[16:24]


def prepare_kernel(basis, weights, index, inverse, scaled, place, names, up_basis, down_basis, blocks):
    width, corners = basis.shape[1], basis.shape[0]
    shared = weights[...] * basis[...]
    scaled[...] = shared
    square = (corners, corners)
    same = lax.broadcasted_iota(jnp.int32, square, 0) == lax.broadcasted_iota(jnp.int32, square, 1)
    column = jnp.sum(jnp.where(same, index[...].astype(F32), 0.0), axis=1, keepdims=True).astype(jnp.int32)
    place[...] = position_of(column)
    named = index[...].astype(F32) + 1.0
    gap = jnp.zeros((1, SLOT_BEFORE - corners), F32)
    row = jnp.concatenate([named, gap, named, gap, named, gap, jnp.zeros((1, SLOT_BEFORE), F32)], axis=1)
    lanes = lax.broadcasted_iota(jnp.int32, (1, LANES), 1)
    names[...] = jnp.where(lanes < corners, row, 0.0)
    first = lax.broadcasted_iota(jnp.int32, (8, LANES), 0) == 0
    for slot, out, rim in ((SLOT_BEFORE, up_basis, shared[:, width - RIM :]), (SLOT_AFTER, down_basis, shared[:, :RIM])):
        out[:corners] = rim
        mine = first & (lanes >= slot) & (lanes < slot + corners)
        told = jnp.where(mine, jnp.broadcast_to(row, (8, LANES)), 0.0)
        out[corners:] = jnp.concatenate([told, jnp.zeros((8, RIM - LANES), F32)], axis=1)
    for q in range(N_COLS):
        blocks[q] = inverse[:, q * LANES : (q + 1) * LANES]


def scatter_kernel(lower, middle, upper, before, after, scaled_basis, place, force, out):
    whole = jnp.concatenate([lower[...] + before[...], middle[...], upper[...] + after[...]], axis=1)
    force[...] = whole
    terms = lax.dot_general(whole, scaled_basis[...], (((1,), (1,)), ((), ())), precision=HIGH, preferred_element_type=F32)
    columns = lax.broadcasted_iota(jnp.int32, (place.shape[0], N_ROWS * LANES), 1)
    hot = (columns == place[...]).astype(F32).astype(BF16)
    dense = added(jnp.dot(three_parts(terms), hot, preferred_element_type=F32))
    for p in range(N_ROWS):
        out[p] = dense[:, p * LANES : (p + 1) * LANES]


def spread_kernel(arrived, out):
    total = jnp.sum(arrived[...], axis=0)
    out[...] = jnp.broadcast_to(total[None], out.shape)


def spread_with_blocks_kernel(arrived, blocks, out):
    total = jnp.sum(arrived[...], axis=0)
    for q in range(N_COLS):
        out[q, 0] = total[0:4]
        out[q, 1] = total[4:8]
        out[q, 2] = blocks[q]


def block_kernel(arrived, out, block):
    total = jnp.concatenate([jnp.sum(arrived[:, 0], axis=0), jnp.sum(arrived[:, 1], axis=0)], axis=0)
    for q in range(N_COLS):
        block[4 * q : 4 * q + 4] = arrived[q, 2]
    value = jnp.dot(total[:, : block.shape[0]], block[...], precision=HIGH, preferred_element_type=F32)
    out[...] = jnp.broadcast_to(value[None], out.shape)


def finish_kernel(value, names, scaled_basis, neumann_part, before, after, schur, solution, applied, held, sems):
    width = neumann_part.shape[1]
    cases, corners = neumann_part.shape[0], scaled_basis.shape[0]
    copies = [
        pltpu.make_async_copy(schur.at[pl.ds(k * RIM, RIM)], held.at[pl.ds(k * RIM, RIM)], sems.at[k])
        for k in range(width // RIM)
    ]
    for copy in copies:
        copy.start()
    last = cases + corners
    wanted = names[...] + before[last : last + 1, :LANES] + after[last : last + 1, :LANES]
    found = jnp.zeros((3 * cases, LANES), F32)
    for q in range(N_COLS):
        rows = lax.broadcasted_iota(jnp.int32, (LANES, LANES), 0) + (q * LANES + 1)
        hot = (rows.astype(F32) == wanted).astype(F32).astype(BF16)
        found += jnp.dot(three_parts(value[q]), hot, preferred_element_type=F32)
    picked = added(found)

    def coarse(slot, basis):
        return jnp.dot(picked[:, slot : slot + corners], basis, precision=HIGH, preferred_element_type=F32)

    u = neumann_part[...] + coarse(0, scaled_basis[...])
    lower = u[:, :RIM] + before[:cases] + coarse(SLOT_BEFORE, before[cases:last])
    upper = u[:, width - RIM :] + after[:cases] + coarse(SLOT_AFTER, after[cases:last])
    u = jnp.concatenate([lower, u[:, RIM : width - RIM], upper], axis=1)
    solution[...] = u
    total = 4.0 * u
    rounded = u.astype(BF16)
    for k, copy in enumerate(copies):
        copy.wait()
        part = rounded[:, k * RIM : (k + 1) * RIM]
        total += jnp.dot(part, held[k * RIM : (k + 1) * RIM], preferred_element_type=F32)
    applied[...] = total


def call(kernel, shapes, *args, in_hbm=(), scratch=(), limit=24 << 20):
    shapes = [s if isinstance(s, jax.ShapeDtypeStruct) else jax.ShapeDtypeStruct(s, F32) for s in shapes]
    return pl.pallas_call(
        kernel,
        out_shape=shapes,
        in_specs=[pl.BlockSpec(memory_space=pltpu.HBM if i in in_hbm else pltpu.VMEM) for i in range(len(args))],
        out_specs=[pl.BlockSpec(memory_space=pltpu.VMEM)] * len(shapes),
        scratch_shapes=list(scratch),
        compiler_params=pltpu.CompilerParams(vmem_limit_bytes=limit),
    )(*args)


def local(loads, schur, neumann, basis, coarse_index, coarse_inverse):
    loads, schur, neumann, basis, index = loads[0], schur[0], neumann[0], basis[0], coarse_index[0]
    cases, width = loads.shape
    corners = basis.shape[0]
    position = lax.axis_index(CHAIN)
    columns = lax.broadcasted_iota(jnp.int32, (1, width), 1)
    lower_rim = (columns < RIM) & (position > 0)
    upper_rim = (columns >= width - RIM) & (position < CHAIN_LENGTH - 1)
    weights = jnp.where(lower_rim | upper_rim, 0.5, 1.0).astype(F32)
    up = [(i, i + 1) for i in range(CHAIN_LENGTH - 1)]
    down = [(j, i) for i, j in up]

    def rims(field):
        before = lax.ppermute(field[:, width - RIM :], CHAIN, up)
        after = lax.ppermute(field[:, :RIM], CHAIN, down)
        return before, after

    def assemble(field):
        before, after = rims(field)
        middle = field[:, RIM : width - RIM]
        return jnp.concatenate([field[:, :RIM] + before, middle, field[:, width - RIM :] + after], axis=1)

    lower, middle, upper = loads[:, :RIM], loads[:, RIM : width - RIM], loads[:, width - RIM :]
    before = lax.ppermute(upper, CHAIN, up)
    after = lax.ppermute(lower, CHAIN, down)
    own = corners + 8
    scaled_basis, place, own_names, up_basis, down_basis, blocks = call(
        prepare_kernel,
        [
            (corners, width), jax.ShapeDtypeStruct((corners, 1), jnp.int32), (1, LANES),
            (own, RIM), (own, RIM), (N_COLS, 4, LANES),
        ],
        basis, weights, index[None], coarse_inverse,
    )
    force, partial = call(
        scatter_kernel, [(cases, width), (N_ROWS, cases, LANES)], lower, middle, upper, before, after, scaled_basis, place
    )
    arrived = exchange(partial, ROWS)
    (sent,) = call(spread_with_blocks_kernel, [(N_COLS, 3, 4, LANES)], arrived, blocks)
    force, sent, weights = lax.optimization_barrier((force, sent, weights))

    weighted = weights * force
    product = jnp.dot(weighted.astype(BF16), neumann, preferred_element_type=F32)
    neumann_part = weights * (0.25 * weighted + 0.0625 * product)
    to_next = jnp.concatenate([neumann_part[:, width - RIM :], up_basis], axis=0)
    to_last = jnp.concatenate([neumann_part[:, :RIM], down_basis], axis=0)
    told_before = lax.ppermute(to_next, CHAIN, up)
    told_after = lax.ppermute(to_last, CHAIN, down)

    arrived = exchange(sent, COLS)
    arrived, told_before, told_after = lax.optimization_barrier((arrived, told_before, told_after))
    (sent,) = call(
        block_kernel, [(N_ROWS, cases, LANES)], arrived, scratch=(pltpu.VMEM((4 * N_COLS, LANES), F32),)
    )
    arrived = exchange(sent, ROWS)
    (sent,) = call(spread_kernel, [(N_COLS, cases, LANES)], arrived)
    value = exchange(sent, COLS)
    u, applied = call(
        finish_kernel, [(cases, width), (cases, width)],
        value, own_names, scaled_basis, neumann_part, told_before, told_after, schur,
        in_hbm=(6,), limit=LIMIT, scratch=(pltpu.VMEM(schur.shape, BF16), pltpu.SemaphoreType.DMA((width // RIM,))),
    )
    residual = force - assemble(applied)
    return (u[None], residual[None])


def solution(mesh):
    whole = Mesh(mesh.devices.reshape(SIZES), ALL)
    specs = tuple(P(ALL, *([None] * n)) for n in (2, 2, 2, 2, 1, 1))
    outs = (P(ALL, None, None), P(ALL, None, None))
    return jax.shard_map(local, mesh=whole, in_specs=specs, out_specs=outs, check_vma=False)
```

```python
import jax
import jax.numpy as jnp
from jax import lax
from jax.experimental import pallas as pl
from jax.experimental.pallas import tpu as pltpu
from jax.sharding import Mesh, PartitionSpec as P


RIM = 256
ALL = ("yh", "x", "c", "z", "yl")
SIZES = (2, 4, 2, 12, 4)
CHAIN = ("z", "yl")
ROWS = ("yh", "x", "yl")
COLS = ("z", "c")
CHAIN_LENGTH = 48
N_ROWS = 32
N_COLS = 24
SLOT_BEFORE = 32
SLOT_AFTER = 64
LANES = 128
HIGH = lax.Precision.HIGHEST
F32 = jnp.float32
BF16 = jnp.bfloat16


def exchange(x, axes):
    return lax.all_to_all(x, axes, split_axis=0, concat_axis=0, tiled=True)


def in_place(x):
    return pltpu.with_memory_space_constraint(x, pltpu.HBM)


def position_of(index):
    owner = index // 4
    group, member = owner // 48, owner % 48
    row_part = (group // 2) * 4 + member % 4
    col_part = (member // 4) * 2 + group % 2
    return row_part * LANES + col_part * 4 + index % 4


def three_parts(x):
    first = x.astype(BF16)
    rest = x - first.astype(F32)
    second = rest.astype(BF16)
    third = (rest - second.astype(F32)).astype(BF16)
    return jnp.concatenate([first.astype(F32), second.astype(F32), third.astype(F32)], axis=0).astype(BF16)


def added(x):
    return x[0:8] + x[8:16] + x[16:24]


def prepare_kernel(
    basis_from, index_from, inverse_from, loads_from, weights, scaled, place, names, up_basis, down_basis, blocks, loads,
    basis, index, inverse, sems,
):
    pairs = ((basis_from, basis), (index_from, index), (loads_from, loads), (inverse_from, inverse))
    copies = [pltpu.make_async_copy(source, target, sems.at[k]) for k, (source, target) in enumerate(pairs)]
    for copy in copies:
        copy.start()
    for copy in copies:
        copy.wait()
    width, corners = basis.shape[1], basis.shape[0]
    shared = weights[...] * basis[...]
    scaled[...] = shared
    square = (corners, corners)
    same = lax.broadcasted_iota(jnp.int32, square, 0) == lax.broadcasted_iota(jnp.int32, square, 1)
    column = jnp.sum(jnp.where(same, index[...].astype(F32), 0.0), axis=1, keepdims=True).astype(jnp.int32)
    place[...] = position_of(column)
    named = index[...].astype(F32) + 1.0
    gap = jnp.zeros((1, SLOT_BEFORE - corners), F32)
    row = jnp.concatenate([named, gap, named, gap, named, gap, jnp.zeros((1, SLOT_BEFORE), F32)], axis=1)
    lanes = lax.broadcasted_iota(jnp.int32, (1, LANES), 1)
    names[...] = jnp.where(lanes < corners, row, 0.0)
    first = lax.broadcasted_iota(jnp.int32, (8, LANES), 0) == 0
    for slot, out, rim in ((SLOT_BEFORE, up_basis, shared[:, width - RIM :]), (SLOT_AFTER, down_basis, shared[:, :RIM])):
        out[:corners] = rim
        mine = first & (lanes >= slot) & (lanes < slot + corners)
        told = jnp.where(mine, jnp.broadcast_to(row, (8, LANES)), 0.0)
        out[corners:] = jnp.concatenate([told, jnp.zeros((8, RIM - LANES), F32)], axis=1)
    for q in range(N_COLS):
        blocks[q] = inverse[:, q * LANES : (q + 1) * LANES]


def sides(odd, far, near):
    flag = odd[...] > 0.5
    return jnp.where(flag, near[...], far[...]), jnp.where(flag, far[...], near[...])


def scatter_kernel(loads, far, near, odd, weights, scaled_basis, place, force, weighted, out):
    width = loads.shape[1]
    before, after = sides(odd, far, near)
    whole = jnp.concatenate(
        [loads[:, :RIM] + before, loads[:, RIM : width - RIM], loads[:, width - RIM :] + after], axis=1
    )
    force[...] = whole
    weighted[...] = weights[...] * whole
    terms = lax.dot_general(whole, scaled_basis[...], (((1,), (1,)), ((), ())), precision=HIGH, preferred_element_type=F32)
    columns = lax.broadcasted_iota(jnp.int32, (place.shape[0], N_ROWS * LANES), 1)
    hot = (columns == place[...]).astype(F32).astype(BF16)
    dense = added(jnp.dot(three_parts(terms), hot, preferred_element_type=F32))
    for p in range(N_ROWS):
        out[p] = dense[:, p * LANES : (p + 1) * LANES]


def streamed_dot(x, matrix, held, sems, meanwhile):
    steps = matrix.shape[0] // RIM
    copies = [
        pltpu.make_async_copy(matrix.at[pl.ds(k * RIM, RIM)], held.at[pl.ds(k * RIM, RIM)], sems.at[k])
        for k in range(steps)
    ]
    for copy in copies:
        copy.start()
    x = meanwhile() if meanwhile else x
    rounded = x.astype(BF16)
    total = None
    for k, copy in enumerate(copies):
        copy.wait()
        part = jnp.dot(rounded[:, k * RIM : (k + 1) * RIM], held[k * RIM : (k + 1) * RIM], preferred_element_type=F32)
        total = part if total is None else total + part
    return x, total


def neumann_kernel(weighted, weights, odd, up_basis, down_basis, neumann, out, to_far, to_near, held, sems):
    width, cases = weighted.shape[1], weighted.shape[0]
    scaled, product = streamed_dot(weighted[...], neumann, held, sems, None)
    result = weights[...] * (0.25 * scaled + 0.0625 * product)
    out[...] = result
    flag = odd[...] > 0.5
    upper, lower = result[:, width - RIM :], result[:, :RIM]
    to_far[:cases] = jnp.where(flag, upper, lower)
    to_near[:cases] = jnp.where(flag, lower, upper)
    to_far[cases:] = jnp.where(flag, up_basis[...], down_basis[...])
    to_near[cases:] = jnp.where(flag, down_basis[...], up_basis[...])


def spread_kernel(arrived, out):
    total = jnp.sum(arrived[...], axis=0)
    out[...] = jnp.broadcast_to(total[None], out.shape)


def spread_with_blocks_kernel(arrived, blocks, out):
    total = jnp.sum(arrived[...], axis=0)
    for q in range(N_COLS):
        out[q, 0] = total[0:4]
        out[q, 1] = total[4:8]
        out[q, 2] = blocks[q]


def block_kernel(arrived, out, block):
    total = jnp.concatenate([jnp.sum(arrived[:, 0], axis=0), jnp.sum(arrived[:, 1], axis=0)], axis=0)
    for q in range(N_COLS):
        block[4 * q : 4 * q + 4] = arrived[q, 2]
    value = jnp.dot(total[:, : block.shape[0]], block[...], precision=HIGH, preferred_element_type=F32)
    out[...] = jnp.broadcast_to(value[None], out.shape)


def finish_kernel(
    value, names, scaled_basis, neumann_part, odd, far, near, schur, solution, applied, to_far, to_near, held, sems
):
    width = neumann_part.shape[1]
    cases, corners = neumann_part.shape[0], scaled_basis.shape[0]
    last = cases + corners

    def assembled():
        before, after = sides(odd, far, near)
        wanted = names[...] + before[last : last + 1, :LANES] + after[last : last + 1, :LANES]
        found = jnp.zeros((3 * cases, LANES), F32)
        for q in range(N_COLS):
            rows = lax.broadcasted_iota(jnp.int32, (LANES, LANES), 0) + (q * LANES + 1)
            hot = (rows.astype(F32) == wanted).astype(F32).astype(BF16)
            found += jnp.dot(three_parts(value[q]), hot, preferred_element_type=F32)
        picked = added(found)

        def coarse(slot, basis):
            return jnp.dot(picked[:, slot : slot + corners], basis, precision=HIGH, preferred_element_type=F32)

        u = neumann_part[...] + coarse(0, scaled_basis[...])
        lower = u[:, :RIM] + before[:cases] + coarse(SLOT_BEFORE, before[cases:last])
        upper = u[:, width - RIM :] + after[:cases] + coarse(SLOT_AFTER, after[cases:last])
        u = jnp.concatenate([lower, u[:, RIM : width - RIM], upper], axis=1)
        solution[...] = u
        return u

    u, product = streamed_dot(None, schur, held, sems, assembled)
    total = 4.0 * u + product
    applied[...] = total
    flag = odd[...] > 0.5
    upper, lower = total[:, width - RIM :], total[:, :RIM]
    to_far[...] = jnp.where(flag, upper, lower)
    to_near[...] = jnp.where(flag, lower, upper)


def call(kernel, shapes, *args, in_hbm=(), scratch=()):
    shapes = [s if isinstance(s, jax.ShapeDtypeStruct) else jax.ShapeDtypeStruct(s, F32) for s in shapes]
    return pl.pallas_call(
        kernel,
        out_shape=shapes,
        in_specs=[pl.BlockSpec(memory_space=pltpu.HBM if i in in_hbm else pltpu.VMEM) for i in range(len(args))],
        out_specs=[pl.BlockSpec(memory_space=pltpu.VMEM)] * len(shapes),
        scratch_shapes=list(scratch),
        compiler_params=pltpu.CompilerParams(vmem_limit_bytes=24 << 20),
    )(*args)


def local(loads, schur, neumann, basis, coarse_index, coarse_inverse):
    loads, schur, neumann, basis, index = loads[0], schur[0], neumann[0], basis[0], coarse_index[0]
    cases, width = loads.shape
    corners = basis.shape[0]
    position = lax.axis_index(CHAIN)
    columns = lax.broadcasted_iota(jnp.int32, (1, width), 1)
    lower_rim = (columns < RIM) & (position > 0)
    upper_rim = (columns >= width - RIM) & (position < CHAIN_LENGTH - 1)
    weights = jnp.where(lower_rim | upper_rim, 0.5, 1.0).astype(F32)
    is_odd = position % 2 == 1
    odd = jnp.broadcast_to(jnp.where(is_odd, 1.0, 0.0).astype(F32), (1, RIM))

    def swap(x, first):
        pairs = [(i, i + 1) for i in range(first, CHAIN_LENGTH - 1, 2)]
        return lax.ppermute(x, CHAIN, pairs + [(j, i) for i, j in pairs])

    lower, upper = loads[:, :RIM], loads[:, width - RIM :]
    far = swap(jnp.where(is_odd, upper, lower), 1)
    near = swap(jnp.where(is_odd, lower, upper), 0)
    own = corners + 8
    streamed = dict(scratch=(pltpu.VMEM(schur.shape, BF16), pltpu.SemaphoreType.DMA((width // RIM,))))
    scaled_basis, place, own_names, up_basis, down_basis, blocks, near_loads = call(
        prepare_kernel,
        [
            (corners, width), jax.ShapeDtypeStruct((corners, 1), jnp.int32), (1, LANES),
            (own, RIM), (own, RIM), (N_COLS, 4, LANES), (cases, width),
        ],
        *(in_place(x) for x in (basis, index[None], coarse_inverse, loads)), weights,
        in_hbm=(0, 1, 2, 3),
        scratch=(
            pltpu.VMEM((corners, width), F32), pltpu.VMEM((1, corners), jnp.int32), pltpu.VMEM(coarse_inverse.shape, F32),
            pltpu.SemaphoreType.DMA((4,)),
        ),
    )
    force, weighted, partial = call(
        scatter_kernel, [(cases, width), (cases, width), (N_ROWS, cases, LANES)],
        near_loads, far, near, odd, weights, scaled_basis, place,
    )
    arrived = exchange(partial, ROWS)
    (sent,) = call(spread_with_blocks_kernel, [(N_COLS, 3, 4, LANES)], arrived, blocks)
    weighted, sent = lax.optimization_barrier((weighted, sent))

    neumann_part, to_far, to_near = call(
        neumann_kernel, [(cases, width), (cases + own, RIM), (cases + own, RIM)],
        weighted, weights, odd, up_basis, down_basis, in_place(neumann), in_hbm=(5,), **streamed,
    )
    told_far = swap(to_far, 1)
    told_near = swap(to_near, 0)

    arrived = exchange(sent, COLS)
    (sent,) = call(
        block_kernel, [(N_ROWS, cases, LANES)], arrived, scratch=(pltpu.VMEM((4 * N_COLS, LANES), F32),)
    )
    arrived = exchange(sent, ROWS)
    (sent,) = call(spread_kernel, [(N_COLS, cases, LANES)], arrived)
    value = exchange(sent, COLS)
    u, applied, to_far, to_near = call(
        finish_kernel, [(cases, width), (cases, width), (cases, RIM), (cases, RIM)],
        value, own_names, scaled_basis, neumann_part, odd, told_far, told_near, in_place(schur), in_hbm=(7,), **streamed,
    )
    far = swap(to_far, 1)
    near = swap(to_near, 0)
    before, after = jnp.where(is_odd, near, far), jnp.where(is_odd, far, near)
    whole = jnp.concatenate(
        [applied[:, :RIM] + before, applied[:, RIM : width - RIM], applied[:, width - RIM :] + after], axis=1
    )
    return (u[None], (force - whole)[None])


def solution(mesh):
    whole = Mesh(mesh.devices.reshape(SIZES), ALL)
    specs = tuple(P(ALL, *([None] * n)) for n in (2, 2, 2, 2, 1, 1))
    outs = (P(ALL, None, None), P(ALL, None, None))
    return jax.shard_map(local, mesh=whole, in_specs=specs, out_specs=outs, check_vma=False)
```

```python
import jax
import jax.numpy as jnp
from jax import lax
from jax.experimental import pallas as pl
from jax.experimental.pallas import tpu as pltpu
from jax.sharding import Mesh, PartitionSpec as P


RIM = 256
ALL = ("yh", "x", "c", "z", "yl")
SIZES = (2, 4, 2, 12, 4)
CHAIN = ("z", "yl")
ROWS = ("yh", "x", "yl")
COLS = ("z", "c")
CHAIN_LENGTH = 48
N_ROWS = 32
N_COLS = 24
SLOT_BEFORE = 32
SLOT_AFTER = 64
LANES = 128
HIGH = lax.Precision.HIGHEST
F32 = jnp.float32
BF16 = jnp.bfloat16


def exchange(x, axes):
    return lax.all_to_all(x, axes, split_axis=0, concat_axis=0, tiled=True)


def in_place(x):
    return pltpu.with_memory_space_constraint(x, pltpu.HBM)


def position_of(index):
    owner = index // 4
    group, member = owner // 48, owner % 48
    row_part = (group // 2) * 4 + member % 4
    col_part = (member // 4) * 2 + group % 2
    return row_part * LANES + col_part * 4 + index % 4


def three_parts(x):
    first = x.astype(BF16)
    rest = x - first.astype(F32)
    second = rest.astype(BF16)
    third = (rest - second.astype(F32)).astype(BF16)
    return jnp.concatenate([first.astype(F32), second.astype(F32), third.astype(F32)], axis=0).astype(BF16)


def added(x):
    return x[0:8] + x[8:16] + x[16:24]


def prepare_kernel(
    basis_from, index_from, inverse_from, loads_from, weights, scaled, place, names, up_basis, down_basis, blocks, loads,
    basis, index, inverse, sems,
):
    pairs = ((basis_from, basis), (index_from, index), (loads_from, loads), (inverse_from, inverse))
    copies = [pltpu.make_async_copy(source, target, sems.at[k]) for k, (source, target) in enumerate(pairs)]
    for copy in copies:
        copy.start()
    for copy in copies:
        copy.wait()
    width, corners = basis.shape[1], basis.shape[0]
    shared = weights[...] * basis[...]
    scaled[...] = shared
    square = (corners, corners)
    same = lax.broadcasted_iota(jnp.int32, square, 0) == lax.broadcasted_iota(jnp.int32, square, 1)
    column = jnp.sum(jnp.where(same, index[...].astype(F32), 0.0), axis=1, keepdims=True).astype(jnp.int32)
    place[...] = position_of(column)
    named = index[...].astype(F32) + 1.0
    gap = jnp.zeros((1, SLOT_BEFORE - corners), F32)
    row = jnp.concatenate([named, gap, named, gap, named, gap, jnp.zeros((1, SLOT_BEFORE), F32)], axis=1)
    lanes = lax.broadcasted_iota(jnp.int32, (1, LANES), 1)
    names[...] = jnp.where(lanes < corners, row, 0.0)
    first = lax.broadcasted_iota(jnp.int32, (8, LANES), 0) == 0
    for slot, out, rim in ((SLOT_BEFORE, up_basis, shared[:, width - RIM :]), (SLOT_AFTER, down_basis, shared[:, :RIM])):
        out[:corners] = rim
        mine = first & (lanes >= slot) & (lanes < slot + corners)
        told = jnp.where(mine, jnp.broadcast_to(row, (8, LANES)), 0.0)
        out[corners:] = jnp.concatenate([told, jnp.zeros((8, RIM - LANES), F32)], axis=1)
    for q in range(N_COLS):
        blocks[q] = inverse[:, q * LANES : (q + 1) * LANES]


def sides(odd, far, near):
    flag = odd[...] > 0.5
    return jnp.where(flag, near[...], far[...]), jnp.where(flag, far[...], near[...])


def scatter_kernel(loads, far, near, odd, weights, scaled_basis, place, force, weighted, out):
    width = loads.shape[1]
    before, after = sides(odd, far, near)
    whole = jnp.concatenate(
        [loads[:, :RIM] + before, loads[:, RIM : width - RIM], loads[:, width - RIM :] + after], axis=1
    )
    force[...] = whole
    weighted[...] = weights[...] * whole
    terms = lax.dot_general(whole, scaled_basis[...], (((1,), (1,)), ((), ())), precision=HIGH, preferred_element_type=F32)
    columns = lax.broadcasted_iota(jnp.int32, (place.shape[0], N_ROWS * LANES), 1)
    hot = (columns == place[...]).astype(F32).astype(BF16)
    dense = added(jnp.dot(three_parts(terms), hot, preferred_element_type=F32))
    for p in range(N_ROWS):
        out[p] = dense[:, p * LANES : (p + 1) * LANES]


def streamed_dot(x, matrix, held, sems):
    copies = [
        pltpu.make_async_copy(matrix.at[pl.ds(k * RIM, RIM)], held.at[pl.ds(k * RIM, RIM)], sems.at[k])
        for k in range(matrix.shape[0] // RIM)
    ]
    for copy in copies:
        copy.start()
    total = None
    for k, copy in enumerate(copies):
        copy.wait()
        part = jnp.dot(x[:, k * RIM : (k + 1) * RIM], held[k * RIM : (k + 1) * RIM], preferred_element_type=F32)
        total = part if total is None else total + part
    return total


def fetch_kernel(matrix, out, sem):
    copy = pltpu.make_async_copy(matrix, out, sem.at[0])
    copy.start()
    copy.wait()


def neumann_kernel(weighted, weights, odd, up_basis, down_basis, neumann, out, to_far, to_near, held, sems):
    width, cases = weighted.shape[1], weighted.shape[0]
    scaled = weighted[...]
    product = streamed_dot(scaled.astype(BF16), neumann, held, sems)
    result = weights[...] * (0.25 * scaled + 0.0625 * product)
    out[...] = result
    flag = odd[...] > 0.5
    upper, lower = result[:, width - RIM :], result[:, :RIM]
    to_far[:cases] = jnp.where(flag, upper, lower)
    to_near[:cases] = jnp.where(flag, lower, upper)
    to_far[cases:] = jnp.where(flag, up_basis[...], down_basis[...])
    to_near[cases:] = jnp.where(flag, down_basis[...], up_basis[...])


def spread_kernel(arrived, out):
    total = jnp.sum(arrived[...], axis=0)
    out[...] = jnp.broadcast_to(total[None], out.shape)


def spread_with_blocks_kernel(arrived, blocks, out):
    total = jnp.sum(arrived[...], axis=0)
    for q in range(N_COLS):
        out[q, 0] = total[0:4]
        out[q, 1] = total[4:8]
        out[q, 2] = blocks[q]


def block_kernel(arrived, out, block):
    total = jnp.concatenate([jnp.sum(arrived[:, 0], axis=0), jnp.sum(arrived[:, 1], axis=0)], axis=0)
    for q in range(N_COLS):
        block[4 * q : 4 * q + 4] = arrived[q, 2]
    value = jnp.dot(total[:, : block.shape[0]], block[...], precision=HIGH, preferred_element_type=F32)
    out[...] = jnp.broadcast_to(value[None], out.shape)


def finish_kernel(
    value, names, scaled_basis, neumann_part, odd, far, near, schur, solution, applied, to_far, to_near
):
    width = neumann_part.shape[1]
    cases, corners = neumann_part.shape[0], scaled_basis.shape[0]
    last = cases + corners

    def assembled():
        before, after = sides(odd, far, near)
        wanted = names[...] + before[last : last + 1, :LANES] + after[last : last + 1, :LANES]
        found = jnp.zeros((3 * cases, LANES), F32)
        for q in range(N_COLS):
            rows = lax.broadcasted_iota(jnp.int32, (LANES, LANES), 0) + (q * LANES + 1)
            hot = (rows.astype(F32) == wanted).astype(F32).astype(BF16)
            found += jnp.dot(three_parts(value[q]), hot, preferred_element_type=F32)
        picked = added(found)

        def coarse(slot, basis):
            return jnp.dot(picked[:, slot : slot + corners], basis, precision=HIGH, preferred_element_type=F32)

        u = neumann_part[...] + coarse(0, scaled_basis[...])
        lower = u[:, :RIM] + before[:cases] + coarse(SLOT_BEFORE, before[cases:last])
        upper = u[:, width - RIM :] + after[:cases] + coarse(SLOT_AFTER, after[cases:last])
        u = jnp.concatenate([lower, u[:, RIM : width - RIM], upper], axis=1)
        solution[...] = u
        return u

    u = assembled()
    total = 4.0 * u + jnp.dot(u.astype(BF16), schur[...], preferred_element_type=F32)
    applied[...] = total
    flag = odd[...] > 0.5
    upper, lower = total[:, width - RIM :], total[:, :RIM]
    to_far[...] = jnp.where(flag, upper, lower)
    to_near[...] = jnp.where(flag, lower, upper)


def call(kernel, shapes, *args, in_hbm=(), scratch=()):
    shapes = [s if isinstance(s, jax.ShapeDtypeStruct) else jax.ShapeDtypeStruct(s, F32) for s in shapes]
    return pl.pallas_call(
        kernel,
        out_shape=shapes,
        in_specs=[pl.BlockSpec(memory_space=pltpu.HBM if i in in_hbm else pltpu.VMEM) for i in range(len(args))],
        out_specs=[pl.BlockSpec(memory_space=pltpu.VMEM)] * len(shapes),
        scratch_shapes=list(scratch),
        compiler_params=pltpu.CompilerParams(vmem_limit_bytes=24 << 20),
    )(*args)


def local(loads, schur, neumann, basis, coarse_index, coarse_inverse):
    loads, schur, neumann, basis, index = loads[0], schur[0], neumann[0], basis[0], coarse_index[0]
    cases, width = loads.shape
    corners = basis.shape[0]
    position = lax.axis_index(CHAIN)
    columns = lax.broadcasted_iota(jnp.int32, (1, width), 1)
    lower_rim = (columns < RIM) & (position > 0)
    upper_rim = (columns >= width - RIM) & (position < CHAIN_LENGTH - 1)
    weights = jnp.where(lower_rim | upper_rim, 0.5, 1.0).astype(F32)
    is_odd = position % 2 == 1
    odd = jnp.broadcast_to(jnp.where(is_odd, 1.0, 0.0).astype(F32), (1, RIM))

    def swap(x, first):
        pairs = [(i, i + 1) for i in range(first, CHAIN_LENGTH - 1, 2)]
        return lax.ppermute(x, CHAIN, pairs + [(j, i) for i, j in pairs])

    lower, upper = loads[:, :RIM], loads[:, width - RIM :]
    far = swap(jnp.where(is_odd, upper, lower), 1)
    near = swap(jnp.where(is_odd, lower, upper), 0)
    own = corners + 8
    streamed = dict(scratch=(pltpu.VMEM(schur.shape, BF16), pltpu.SemaphoreType.DMA((width // RIM,))))
    scaled_basis, place, own_names, up_basis, down_basis, blocks, near_loads = call(
        prepare_kernel,
        [
            (corners, width), jax.ShapeDtypeStruct((corners, 1), jnp.int32), (1, LANES),
            (own, RIM), (own, RIM), (N_COLS, 4, LANES), (cases, width),
        ],
        *(in_place(x) for x in (basis, index[None], coarse_inverse, loads)), weights,
        in_hbm=(0, 1, 2, 3),
        scratch=(
            pltpu.VMEM((corners, width), F32), pltpu.VMEM((1, corners), jnp.int32), pltpu.VMEM(coarse_inverse.shape, F32),
            pltpu.SemaphoreType.DMA((4,)),
        ),
    )
    force, weighted, partial = call(
        scatter_kernel, [(cases, width), (cases, width), (N_ROWS, cases, LANES)],
        near_loads, far, near, odd, weights, scaled_basis, place,
    )
    arrived = exchange(partial, ROWS)
    (sent,) = call(spread_with_blocks_kernel, [(N_COLS, 3, 4, LANES)], arrived, blocks)
    weighted, sent = lax.optimization_barrier((weighted, sent))

    neumann_part, to_far, to_near = call(
        neumann_kernel, [(cases, width), (cases + own, RIM), (cases + own, RIM)],
        weighted, weights, odd, up_basis, down_basis, in_place(neumann), in_hbm=(5,), **streamed,
    )
    told_far = swap(to_far, 1)
    told_near = swap(to_near, 0)

    (fetched,) = call(
        fetch_kernel, [jax.ShapeDtypeStruct(schur.shape, BF16)], in_place(schur), in_hbm=(0,),
        scratch=(pltpu.SemaphoreType.DMA((1,)),),
    )
    arrived = exchange(sent, COLS)
    arrived, told_far, told_near = lax.optimization_barrier((arrived, told_far, told_near))
    (sent,) = call(
        block_kernel, [(N_ROWS, cases, LANES)], arrived, scratch=(pltpu.VMEM((4 * N_COLS, LANES), F32),)
    )
    arrived = exchange(sent, ROWS)
    (sent,) = call(spread_kernel, [(N_COLS, cases, LANES)], arrived)
    value = exchange(sent, COLS)
    u, applied, to_far, to_near = call(
        finish_kernel, [(cases, width), (cases, width), (cases, RIM), (cases, RIM)],
        value, own_names, scaled_basis, neumann_part, odd, told_far, told_near, fetched,
    )
    far = swap(to_far, 1)
    near = swap(to_near, 0)
    before, after = jnp.where(is_odd, near, far), jnp.where(is_odd, far, near)
    whole = jnp.concatenate(
        [applied[:, :RIM] + before, applied[:, RIM : width - RIM], applied[:, width - RIM :] + after], axis=1
    )
    return (u[None], (force - whole)[None])


def solution(mesh):
    whole = Mesh(mesh.devices.reshape(SIZES), ALL)
    specs = tuple(P(ALL, *([None] * n)) for n in (2, 2, 2, 2, 1, 1))
    outs = (P(ALL, None, None), P(ALL, None, None))
    return jax.shard_map(local, mesh=whole, in_specs=specs, out_specs=outs, check_vma=False)
```

```python
import jax
import jax.numpy as jnp
from jax import lax
from jax.experimental import pallas as pl
from jax.experimental.pallas import tpu as pltpu
from jax.sharding import Mesh, PartitionSpec as P


RIM = 256
ALL = ("yh", "x", "c", "z", "yl")
SIZES = (2, 4, 2, 12, 4)
CHAIN = ("z", "yl")
ROWS = ("yh", "x", "yl")
COLS = ("z", "c")
CHAIN_LENGTH = 48
N_ROWS = 32
N_COLS = 24
SLOT_BEFORE = 32
SLOT_AFTER = 64
LANES = 128
HIGH = lax.Precision.HIGHEST
F32 = jnp.float32
BF16 = jnp.bfloat16


def exchange(x, axes):
    return lax.all_to_all(x, axes, split_axis=0, concat_axis=0, tiled=True)


def in_place(x):
    return pltpu.with_memory_space_constraint(x, pltpu.HBM)


def position_of(index):
    owner = index // 4
    group, member = owner // 48, owner % 48
    row_part = (group // 2) * 4 + member % 4
    col_part = (member // 4) * 2 + group % 2
    return row_part * LANES + col_part * 4 + index % 4


def three_parts(x):
    first = x.astype(BF16)
    rest = x - first.astype(F32)
    second = rest.astype(BF16)
    third = (rest - second.astype(F32)).astype(BF16)
    return jnp.concatenate([first.astype(F32), second.astype(F32), third.astype(F32)], axis=0).astype(BF16)


def added(x):
    return x[0:8] + x[8:16] + x[16:24]


def prepare_kernel(
    basis_from, index_from, inverse_from, loads_from, weights, scaled, place, names, up_basis, down_basis, blocks, loads,
    basis, index, inverse, sems,
):
    pairs = ((basis_from, basis), (index_from, index), (loads_from, loads), (inverse_from, inverse))
    copies = [pltpu.make_async_copy(source, target, sems.at[k]) for k, (source, target) in enumerate(pairs)]
    for copy in copies:
        copy.start()
    for copy in copies:
        copy.wait()
    width, corners = basis.shape[1], basis.shape[0]
    shared = weights[...] * basis[...]
    scaled[...] = shared
    square = (corners, corners)
    same = lax.broadcasted_iota(jnp.int32, square, 0) == lax.broadcasted_iota(jnp.int32, square, 1)
    column = jnp.sum(jnp.where(same, index[...].astype(F32), 0.0), axis=1, keepdims=True).astype(jnp.int32)
    place[...] = position_of(column)
    named = index[...].astype(F32) + 1.0
    gap = jnp.zeros((1, SLOT_BEFORE - corners), F32)
    row = jnp.concatenate([named, gap, named, gap, named, gap, jnp.zeros((1, SLOT_BEFORE), F32)], axis=1)
    lanes = lax.broadcasted_iota(jnp.int32, (1, LANES), 1)
    names[...] = jnp.where(lanes < corners, row, 0.0)
    first = lax.broadcasted_iota(jnp.int32, (8, LANES), 0) == 0
    for slot, out, rim in ((SLOT_BEFORE, up_basis, shared[:, width - RIM :]), (SLOT_AFTER, down_basis, shared[:, :RIM])):
        out[:corners] = rim
        mine = first & (lanes >= slot) & (lanes < slot + corners)
        told = jnp.where(mine, jnp.broadcast_to(row, (8, LANES)), 0.0)
        out[corners:] = jnp.concatenate([told, jnp.zeros((8, RIM - LANES), F32)], axis=1)
    for q in range(N_COLS):
        blocks[q] = inverse[:, q * LANES : (q + 1) * LANES]


def sides(odd, far, near):
    flag = odd[...] > 0.5
    return jnp.where(flag, near[...], far[...]), jnp.where(flag, far[...], near[...])


def scatter_kernel(loads, far, near, odd, weights, scaled_basis, place, force, weighted, out):
    width = loads.shape[1]
    before, after = sides(odd, far, near)
    whole = jnp.concatenate(
        [loads[:, :RIM] + before, loads[:, RIM : width - RIM], loads[:, width - RIM :] + after], axis=1
    )
    force[...] = whole
    weighted[...] = weights[...] * whole
    terms = lax.dot_general(whole, scaled_basis[...], (((1,), (1,)), ((), ())), precision=HIGH, preferred_element_type=F32)
    columns = lax.broadcasted_iota(jnp.int32, (place.shape[0], N_ROWS * LANES), 1)
    hot = (columns == place[...]).astype(F32).astype(BF16)
    dense = added(jnp.dot(three_parts(terms), hot, preferred_element_type=F32))
    for p in range(N_ROWS):
        out[p] = dense[:, p * LANES : (p + 1) * LANES]


def streamed_dot(x, matrix, held, sems):
    copies = [
        pltpu.make_async_copy(matrix.at[pl.ds(k * RIM, RIM)], held.at[pl.ds(k * RIM, RIM)], sems.at[k])
        for k in range(matrix.shape[0] // RIM)
    ]
    for copy in copies:
        copy.start()
    total = None
    for k, copy in enumerate(copies):
        copy.wait()
        part = jnp.dot(x[:, k * RIM : (k + 1) * RIM], held[k * RIM : (k + 1) * RIM], preferred_element_type=F32)
        total = part if total is None else total + part
    return total


def fetch_kernel(matrix, out, sem):
    copy = pltpu.make_async_copy(matrix, out, sem.at[0])
    copy.start()
    copy.wait()


def neumann_kernel(weighted, weights, odd, up_basis, down_basis, neumann, out, to_far, to_near, held, sems):
    width, cases = weighted.shape[1], weighted.shape[0]
    scaled = weighted[...]
    product = streamed_dot(scaled.astype(BF16), neumann, held, sems)
    result = weights[...] * (0.25 * scaled + 0.0625 * product)
    out[...] = result
    flag = odd[...] > 0.5
    upper, lower = result[:, width - RIM :], result[:, :RIM]
    to_far[:cases] = jnp.where(flag, upper, lower)
    to_near[:cases] = jnp.where(flag, lower, upper)
    to_far[cases:] = jnp.where(flag, up_basis[...], down_basis[...])
    to_near[cases:] = jnp.where(flag, down_basis[...], up_basis[...])


def spread_kernel(arrived, out):
    total = jnp.sum(arrived[...], axis=0)
    out[...] = jnp.broadcast_to(total[None], out.shape)


def spread_with_blocks_kernel(arrived, blocks, out):
    total = jnp.sum(arrived[...], axis=0)
    for q in range(N_COLS):
        out[q, 0] = total[0:4]
        out[q, 1] = total[4:8]
        out[q, 2] = blocks[q]


def block_kernel(arrived, out, block):
    total = jnp.concatenate([jnp.sum(arrived[:, 0], axis=0), jnp.sum(arrived[:, 1], axis=0)], axis=0)
    for q in range(N_COLS):
        block[4 * q : 4 * q + 4] = arrived[q, 2]
    value = jnp.dot(total[:, : block.shape[0]], block[...], precision=HIGH, preferred_element_type=F32)
    out[...] = jnp.broadcast_to(value[None], out.shape)


def finish_kernel(
    value, names, scaled_basis, neumann_part, odd, far, near, schur, solution, applied, to_far, to_near
):
    width = neumann_part.shape[1]
    cases, corners = neumann_part.shape[0], scaled_basis.shape[0]
    last = cases + corners

    def assembled():
        before, after = sides(odd, far, near)
        wanted = names[...] + before[last : last + 1, :LANES] + after[last : last + 1, :LANES]
        found = jnp.zeros((3 * cases, LANES), F32)
        for q in range(N_COLS):
            rows = lax.broadcasted_iota(jnp.int32, (LANES, LANES), 0) + (q * LANES + 1)
            hot = (rows.astype(F32) == wanted).astype(F32).astype(BF16)
            found += jnp.dot(three_parts(value[q]), hot, preferred_element_type=F32)
        picked = added(found)

        def coarse(slot, basis):
            return jnp.dot(picked[:, slot : slot + corners], basis, precision=HIGH, preferred_element_type=F32)

        u = neumann_part[...] + coarse(0, scaled_basis[...])
        lower = u[:, :RIM] + before[:cases] + coarse(SLOT_BEFORE, before[cases:last])
        upper = u[:, width - RIM :] + after[:cases] + coarse(SLOT_AFTER, after[cases:last])
        u = jnp.concatenate([lower, u[:, RIM : width - RIM], upper], axis=1)
        solution[...] = u
        return u

    u = assembled()
    total = 4.0 * u + jnp.dot(u.astype(BF16), schur[...], preferred_element_type=F32)
    applied[...] = total
    flag = odd[...] > 0.5
    upper, lower = total[:, width - RIM :], total[:, :RIM]
    to_far[...] = jnp.where(flag, upper, lower)
    to_near[...] = jnp.where(flag, lower, upper)


def call(kernel, shapes, *args, in_hbm=(), scratch=()):
    shapes = [s if isinstance(s, jax.ShapeDtypeStruct) else jax.ShapeDtypeStruct(s, F32) for s in shapes]
    return pl.pallas_call(
        kernel,
        out_shape=shapes,
        in_specs=[pl.BlockSpec(memory_space=pltpu.HBM if i in in_hbm else pltpu.VMEM) for i in range(len(args))],
        out_specs=[pl.BlockSpec(memory_space=pltpu.VMEM)] * len(shapes),
        scratch_shapes=list(scratch),
        compiler_params=pltpu.CompilerParams(vmem_limit_bytes=24 << 20),
    )(*args)


def local(loads, schur, neumann, basis, coarse_index, coarse_inverse):
    loads, schur, neumann, basis, index = loads[0], schur[0], neumann[0], basis[0], coarse_index[0]
    cases, width = loads.shape
    corners = basis.shape[0]
    position = lax.axis_index(CHAIN)
    columns = lax.broadcasted_iota(jnp.int32, (1, width), 1)
    lower_rim = (columns < RIM) & (position > 0)
    upper_rim = (columns >= width - RIM) & (position < CHAIN_LENGTH - 1)
    weights = jnp.where(lower_rim | upper_rim, 0.5, 1.0).astype(F32)
    is_odd = position % 2 == 1
    odd = jnp.broadcast_to(jnp.where(is_odd, 1.0, 0.0).astype(F32), (1, RIM))

    def swap(x, first):
        pairs = [(i, i + 1) for i in range(first, CHAIN_LENGTH - 1, 2)]
        return lax.ppermute(x, CHAIN, pairs + [(j, i) for i, j in pairs])

    lower, upper = loads[:, :RIM], loads[:, width - RIM :]
    far = swap(jnp.where(is_odd, upper, lower), 1)
    near = swap(jnp.where(is_odd, lower, upper), 0)
    own = corners + 8
    streamed = dict(scratch=(pltpu.VMEM(schur.shape, BF16), pltpu.SemaphoreType.DMA((width // RIM,))))
    shapes = [
        (corners, width), jax.ShapeDtypeStruct((corners, 1), jnp.int32), (1, LANES),
        (own, RIM), (own, RIM), (N_COLS, 4, LANES), (cases, width),
    ]
    scaled_basis, place, own_names, up_basis, down_basis, blocks, near_loads = call(
        prepare_kernel, shapes,
        *(in_place(x) for x in (basis, index[None], coarse_inverse, loads)), weights,
        in_hbm=(0, 1, 2, 3),
        scratch=(
            pltpu.VMEM((corners, width), F32), pltpu.VMEM((1, corners), jnp.int32), pltpu.VMEM(coarse_inverse.shape, F32),
            pltpu.SemaphoreType.DMA((4,)),
        ),
    )
    force, weighted, partial = call(
        scatter_kernel, [(cases, width), (cases, width), (N_ROWS, cases, LANES)],
        near_loads, far, near, odd, weights, scaled_basis, place,
    )
    arrived = exchange(partial, ROWS)
    (sent,) = call(spread_with_blocks_kernel, [(N_COLS, 3, 4, LANES)], arrived, blocks)
    weighted, sent = lax.optimization_barrier((weighted, sent))

    neumann_part, to_far, to_near = call(
        neumann_kernel, [(cases, width), (cases + own, RIM), (cases + own, RIM)],
        weighted, weights, odd, up_basis, down_basis, in_place(neumann), in_hbm=(5,), **streamed,
    )
    told_far = swap(to_far, 1)
    told_near = swap(to_near, 0)

    (fetched,) = call(
        fetch_kernel, [jax.ShapeDtypeStruct(schur.shape, BF16)], in_place(schur), in_hbm=(0,),
        scratch=(pltpu.SemaphoreType.DMA((1,)),),
    )
    arrived = exchange(sent, COLS)
    (sent,) = call(
        block_kernel, [(N_ROWS, cases, LANES)], arrived, scratch=(pltpu.VMEM((4 * N_COLS, LANES), F32),)
    )
    arrived = exchange(sent, ROWS)
    (sent,) = call(spread_kernel, [(N_COLS, cases, LANES)], arrived)
    value = exchange(sent, COLS)
    u, applied, to_far, to_near = call(
        finish_kernel, [(cases, width), (cases, width), (cases, RIM), (cases, RIM)],
        value, own_names, scaled_basis, neumann_part, odd, told_far, told_near, fetched,
    )
    far = swap(to_far, 1)
    near = swap(to_near, 0)
    before, after = jnp.where(is_odd, near, far), jnp.where(is_odd, far, near)
    whole = jnp.concatenate(
        [applied[:, :RIM] + before, applied[:, RIM : width - RIM], applied[:, width - RIM :] + after], axis=1
    )
    return (u[None], (force - whole)[None])


def solution(mesh):
    whole = Mesh(mesh.devices.reshape(SIZES), ALL)
    specs = tuple(P(ALL, *([None] * n)) for n in (2, 2, 2, 2, 1, 1))
    outs = (P(ALL, None, None), P(ALL, None, None))
    return jax.shard_map(local, mesh=whole, in_specs=specs, out_specs=outs, check_vma=False)
```
